32 devices in a mesh: worker: 8 (over z, core), tensor: 4 (over y, x).
Axes of the slice: x: 2, y: 2, z: 4, core: 2. Of those that a mesh axis runs over, the one named last changes fastest.
Arguments:
- hidden_rows: bfloat16 [8, 512, 3584], P('worker', 'tensor'), may hold values from -6 to 6
- document_ids: int32 [8, 512], P('worker'), may hold values from 0 to 7, never falling along the last dimension, each value on 1 to 256 neighbouring positions
- cotangent: bfloat16 [8, 16, 64, 512], P('worker', None, 'tensor'), may hold values from -16 to 16
- partner_map: int32 [8], replicated, may hold values from 0 to 7, as said below
- inner_weights: bfloat16 [8, 16, 64, 3584], P('worker', None, 'tensor'), may hold values from -6 to 6
- first_moment: float32 [8, 16, 64, 3584], P('worker', None, 'tensor'), may hold values from -0.00021362305 to 0.00021362305
- second_moment: float32 [8, 16, 64, 3584], P('worker', None, 'tensor'), may hold values from 5e-10 to 5e-09
- outer_weights: bfloat16 [8, 16, 64, 3584], P('worker', None, 'tensor'), may hold values from -6 to 6
- outer_momentum: bfloat16 [8, 16, 64, 3584], P('worker', None, 'tensor'), may hold values from -1.5 to 1.5
Outputs:
- projected: bfloat16 [8, 16, 64, 512], P('worker', None, 'tensor')
- momentum_next: bfloat16 [8, 16, 64, 3584], P('worker', None, 'tensor')
The draws below stay inside these ranges and needn't reach their ends.
Inputs may be any that keep to these rules, and one draw needn't show every extreme that they name: partner_map is an involution without fixed points: partner_map[partner_map[w]] = w and partner_map[w] != w. document_ids never fall along a sequence.
All inputs are finite; a program needn't handle non-finite values.
Results may differ from the reference program's by a relative error of at most 0.0046.
Values may be sent and summed in bfloat16 or wider, within the bound.
No kernel may reach another device: no remote copies, remote signals or barrier semaphores. Data moves between devices by JAX's collectives and lax.ppermute only.
A program may use at most 128 MiB of HBM per device.

```python
import math
import jax
import jax.numpy as jnp
import numpy as np
from jax import lax

D = 3584
KV_HEADS = 4
PAIRS = 64
BLOCKS = 16
SEQ = 512
WORKERS = 8


def draw_cotangent(key, part):
    ramp = jnp.arange(PAIRS, dtype=jnp.float32) / (PAIRS - 1)
    base = jax.random.truncated_normal(key, -4.0, 4.0, (WORKERS, BLOCKS, PAIRS, SEQ), jnp.float32)
    scale = jnp.exp(ramp * jnp.float32(1.0986))
    return (base * scale[:, None]).astype(jnp.bfloat16)


def draw_partner_map(key, part):
    order = jax.random.permutation(key, WORKERS).astype(jnp.int32)
    evens = order[0::2]
    odds = order[1::2]
    mapping = jnp.zeros((WORKERS,), jnp.int32)
    mapping = mapping.at[evens].set(odds)
    mapping = mapping.at[odds].set(evens)
    return mapping


def levels(stream_key, extent, pieces, low, high):
    def one(axis_at, shards_of):
        heights = jax.random.uniform(jax.random.fold_in(jax.random.fold_in(stream_key, 6), axis_at), (shards_of,), jnp.float32, low / len(pieces), high / len(pieces))
        return jnp.repeat(jnp.exp(heights), extent[axis_at] // shards_of).reshape((-1,) + (1,) * (len(extent) - axis_at - 1))

    factor_of = one(*pieces[0])
    for cut in pieces[1:]:
        factor_of = factor_of * one(*cut)
    return factor_of


def split_up(amount, total, reach, slope):
    loads = [(1 << 20) // math.isqrt(standing ** slope) + 1 for standing in range(2, amount + 1)]
    surplus, holding = total - reach - (amount - 1), [1] * (amount - 1)
    while surplus > 0:
        candidates = [i for i in range(amount - 1) if holding[i] < reach]
        whole, remaining = sum([loads[i] for i in candidates]), surplus
        for i in candidates:
            extra = min(reach - holding[i], max(1, remaining * loads[i] // whole), surplus)
            holding[i] = holding[i] + extra
            surplus = surplus - extra
    return np.array([reach] + holding)


def ragged_sizes(key, amount, total, most, skew):
    if amount == 2:
        one = jax.random.randint(key, (), max(1, total - most), min(most, total - 1) + 1)
        return jnp.stack([one, total - one])
    lengths = jnp.asarray(split_up(amount, total, most, skew), jnp.int32)
    twos = (amount - 1) // 2
    source_of, receiver = lengths[1:1 + 2 * twos:2], lengths[2:2 + 2 * twos:2]
    room = jnp.minimum(source_of - 1, most - receiver)
    passed = jax.random.randint(jax.random.fold_in(key, 1), (twos,), 0, 1 << 20) % (room + 1)
    lengths = lengths.at[1:1 + 2 * twos:2].set(source_of - passed).at[2:2 + 2 * twos:2].set(receiver + passed)
    return lengths[jax.random.permutation(jax.random.fold_in(key, 2), amount)]


def bell_draw(rng, dims, deviation, most, cuts=(), held_as=jnp.bfloat16):
    factor_of = levels(rng, dims, cuts, -0.22, 0.18) if cuts else 1.0
    values = jax.random.normal(rng, dims, jnp.float32) * deviation * factor_of
    return jnp.minimum(jnp.maximum(values, -most), most).astype(held_as)


def setup_inputs(seed: int = 0) -> dict:
    seeds = jax.random.split(jax.random.key(seed), 10)
    hidden_rows = bell_draw(seeds[0], (WORKERS, SEQ, D), 1.0, 6.0, ((0, 8), (1, 4)))
    document_ids = jax.vmap(lambda own: jnp.searchsorted(jnp.cumsum(ragged_sizes(own, 8, SEQ, SEQ // 2, 2)), jnp.arange(SEQ), side="right"))(jax.random.split(seeds[1], WORKERS)).reshape((WORKERS, SEQ)).astype(jnp.int32)
    cotangent = draw_cotangent(jax.random.fold_in(seeds[9], 71), 0)
    partner_map = draw_partner_map(jax.random.fold_in(seeds[9], 71), 0)
    inner_weights = bell_draw(seeds[4], (WORKERS, BLOCKS, PAIRS, D), 1.0, 6.0, ((0, 8), (2, 4)))
    first_moment = bell_draw(seeds[5], (WORKERS, BLOCKS, PAIRS, D), 0.000015, 0.00021362305, ((0, 8), (2, 4)), jnp.float32)
    second_moment = jnp.clip(jnp.exp(math.log(4.999999969612645e-09) - 2.3025851 * jax.random.uniform(seeds[6], (WORKERS, BLOCKS, PAIRS, D), jnp.float32) ** levels(seeds[6], (WORKERS, BLOCKS, PAIRS, D), ((0, 8), (2, 4)), -0.2, 0.2)), 4.999999858590343e-10, 4.999999969612645e-09)
    outer_weights = bell_draw(seeds[7], (WORKERS, BLOCKS, PAIRS, D), 1.0, 6.0, ((0, 8), (2, 4)))
    outer_momentum = bell_draw(seeds[8], (WORKERS, BLOCKS, PAIRS, D), 0.1, 1.5, ((0, 8), (2, 4)))
    return {"hidden_rows": hidden_rows, "document_ids": document_ids, "cotangent": cotangent, "partner_map": partner_map, "inner_weights": inner_weights, "first_moment": first_moment, "second_moment": second_moment, "outer_weights": outer_weights, "outer_momentum": outer_momentum}


rope_base = 1000000.0
clip_norm = 1.0
learn_rate = 0.5
decay_rate = 0.1
bias_first = 1.0
bias_second = 0.632304575
outer_alpha = 0.5
outer_beta = 0.7
outer_gamma = 0.5

def rope_tables(identity, first_pair, count):
    length = identity.shape[0]
    index = jnp.arange(length, dtype=jnp.int32)
    change = jnp.concatenate([jnp.ones((1,), dtype=bool), identity[1:] != identity[:-1]])
    starts = lax.cummax(jnp.where(change, index, jnp.zeros_like(index)), axis=0)
    position = (index - starts).astype(jnp.float32)
    pairs = (first_pair + jnp.arange(count, dtype=jnp.int32)).astype(jnp.float32)
    freq = jnp.exp(pairs * jnp.float32(-math.log(rope_base) / PAIRS))
    angle = freq[:, None] * position[None, :]
    return (jnp.cos(angle), jnp.sin(angle))

def rotate(values, cosine, sine, forward):
    count, length = (values.shape[1], values.shape[2])
    parts = values.reshape(2, KV_HEADS, 2, count, length)
    first = parts[0, :, 0]
    second = parts[0, :, 1]
    cos_b = cosine[None]
    sin_b = sine[None]
    if forward:
        new_first = first * cos_b - second * sin_b
        new_second = second * cos_b + first * sin_b
    else:
        new_first = first * cos_b + second * sin_b
        new_second = second * cos_b - first * sin_b
    keys = jnp.stack([new_first, new_second], axis=1)
    return jnp.concatenate([keys[None], parts[1:2]], axis=0).reshape(BLOCKS, count, length)

def one_worker(items):
    rows, identity, cotangent, theta, moment_one, moment_two, outer = items
    columns = BLOCKS * PAIRS
    scale = D ** (-0.5)
    cosine, sine = rope_tables(identity, 0, PAIRS)
    weights = theta.reshape(columns, D)
    raw = lax.dot_general(weights, rows, (((1,), (1,)), ((), ())), preferred_element_type=jnp.float32) * scale
    projected = rotate(raw.reshape(BLOCKS, PAIRS, SEQ), cosine, sine, True).astype(jnp.bfloat16)
    dz = rotate(cotangent.astype(jnp.float32), cosine, sine, False).astype(jnp.bfloat16).reshape(columns, SEQ)
    grad = jnp.dot(dz, rows, preferred_element_type=jnp.float32) * scale
    total = jnp.sum(grad * grad)
    factor = jnp.minimum(jnp.float32(1.0), clip_norm / (jnp.sqrt(total) + 1e-06))
    clipped = grad * factor
    moment_new = 0.9 * moment_one.reshape(columns, D) + 0.1 * clipped
    second_new = 0.999 * moment_two.reshape(columns, D) + 0.001 * clipped * clipped
    update = moment_new / bias_first / (jnp.sqrt(second_new / bias_second) + 1e-08)
    old = weights.astype(jnp.float32)
    theta_new = old - learn_rate * (update + decay_rate * old)
    pseudo = (outer.reshape(columns, D).astype(jnp.float32) - theta_new).astype(jnp.bfloat16)
    return (projected, pseudo)

def reference(hidden_rows, document_ids, cotangent, partner_map, inner_weights, first_moment, second_moment, outer_weights, outer_momentum):
    projected, pseudo = lax.map(one_worker, (hidden_rows, document_ids, cotangent, inner_weights, first_moment, second_moment, outer_weights))
    outer = outer_weights.reshape(WORKERS, BLOCKS * PAIRS, D).astype(jnp.float32)
    pseudo_own = pseudo.astype(jnp.float32)
    pseudo_mate = jnp.take(pseudo_own, partner_map, axis=0)
    outer_mate = jnp.take(outer, partner_map, axis=0)
    moment = outer_momentum.reshape(WORKERS, BLOCKS * PAIRS, D).astype(jnp.float32)
    result = outer_alpha * moment - outer_beta * (pseudo_own + pseudo_mate) / 2.0 - outer_gamma * (outer - outer_mate) / 2.0
    return (projected, result.astype(jnp.bfloat16).reshape(WORKERS, BLOCKS, PAIRS, D))
```

```python
import functools
import math

import jax
import jax.numpy as jnp
from jax import lax
from jax.sharding import PartitionSpec as P

KV_HEADS = 4
PAIRS = 64
BLOCKS = 16


rope_base = 1000000.0
clip_norm = 1.0
learn_rate = 0.5
decay_rate = 0.1
bias_first = 1.0
bias_second = 0.632304575
outer_alpha = 0.5
outer_beta = 0.7
outer_gamma = 0.5


def rope_tables(identity, first_pair, count):
    length = identity.shape[0]
    index = jnp.arange(length, dtype=jnp.int32)
    change = jnp.concatenate([jnp.ones((1,), dtype=bool), identity[1:] != identity[:-1]])
    starts = lax.cummax(jnp.where(change, index, jnp.zeros_like(index)), axis=0)
    position = (index - starts).astype(jnp.float32)
    pairs = (first_pair + jnp.arange(count, dtype=jnp.int32)).astype(jnp.float32)
    freq = jnp.exp(pairs * jnp.float32(-math.log(rope_base) / PAIRS))
    angle = freq[:, None] * position[None, :]
    return (jnp.cos(angle), jnp.sin(angle))


def rotate(values, cosine, sine, forward):
    count, length = (values.shape[1], values.shape[2])
    parts = values.reshape(2, KV_HEADS, 2, count, length)
    first = parts[0, :, 0]
    second = parts[0, :, 1]
    cos_b = cosine[None]
    sin_b = sine[None]
    if forward:
        new_first = first * cos_b - second * sin_b
        new_second = second * cos_b + first * sin_b
    else:
        new_first = first * cos_b + second * sin_b
        new_second = second * cos_b - first * sin_b
    keys = jnp.stack([new_first, new_second], axis=1)
    return jnp.concatenate([keys[None], parts[1:2]], axis=0).reshape(BLOCKS, count, length)


CHUNKS = 4


def send(values, axis, flip):
    return lax.ppermute(values, axis, [(i, i ^ flip) for i in range(lax.axis_size(axis))])


def reorder(values, place):
    parts = jnp.split(values, 4, axis=-1)
    odd = (place & 1) == 1
    high = (place & 2) == 2
    parts = [jnp.where(odd, parts[k ^ 1], parts[k]) for k in range(4)]
    parts = [jnp.where(high, parts[k ^ 2], parts[k]) for k in range(4)]
    return jnp.concatenate(parts, axis=-1)


def tensor_sum(value):
    size = lax.axis_size("tensor")
    if size & (size - 1):
        return lax.psum(value, "tensor")
    flip = 1
    while flip < size:
        value = value + send(value, "tensor", flip)
        flip *= 2
    return value


def per_device(
    hidden_rows,
    document_ids,
    cotangent,
    partner_map,
    inner_weights,
    first_moment,
    second_moment,
    outer_weights,
    outer_momentum,
):
    local_pairs = cotangent.shape[2]
    length = cotangent.shape[3]
    width = hidden_rows.shape[2]
    columns = BLOCKS * local_pairs
    scale = width ** (-0.5)
    shards = lax.axis_size("tensor")
    workers = lax.axis_size("worker")
    place = lax.axis_index("tensor")
    me = lax.axis_index("worker")
    ring = shards == 4

    hidden = hidden_rows[0]
    if ring:
        half = hidden.shape[0] // 2
        low, high = hidden[:half], hidden[half:]
        x_low = send(low, "tensor", 1)
        y_high = send(high, "tensor", 2)
        x_high = send(high, "tensor", 1)
        y_low = send(low, "tensor", 2)
        d_low = send(x_low, "tensor", 2)
        d_high = send(y_high, "tensor", 1)
        near = jnp.concatenate([hidden, x_low, x_high, y_low, y_high], axis=0)
        far = jnp.concatenate([d_low, d_high], axis=0)
    else:
        near = lax.all_gather(hidden, "tensor", axis=0, tiled=True)
        far = None

    cosine, sine = rope_tables(document_ids[0], place * local_pairs, local_pairs)
    dz = (
        rotate(cotangent[0].astype(jnp.float32), cosine, sine, False)
        .astype(jnp.bfloat16)
        .reshape(columns, length)
    )
    if ring:
        dz = reorder(dz, place)
    split = near.shape[0]
    grad = jnp.dot(dz[:, :split], near, preferred_element_type=jnp.float32)
    if far is not None:
        grad = grad + jnp.dot(dz[:, split:], far, preferred_element_type=jnp.float32)
    grad = grad * scale
    total = tensor_sum(jnp.sum(grad * grad))
    factor = jnp.minimum(jnp.float32(1.0), clip_norm / (jnp.sqrt(total) + 1e-06))

    weights = inner_weights[0].reshape(columns, width)
    outer = outer_weights[0].reshape(columns, width)
    momentum = outer_momentum[0].reshape(columns, width)
    moment_one = first_moment[0].reshape(columns, width)
    moment_two = second_moment[0].reshape(columns, width)

    clipped = grad * factor
    moment_new = 0.9 * moment_one + 0.1 * clipped
    second_new = 0.999 * moment_two + 0.001 * clipped * clipped
    update = moment_new / bias_first / (jnp.sqrt(second_new / bias_second) + 1e-08)
    old = weights.astype(jnp.float32)
    theta_new = old - learn_rate * (update + decay_rate * old)
    outer_own = outer.astype(jnp.float32)
    pseudo = (outer_own - theta_new).astype(jnp.bfloat16)
    mine = (
        0.5 * outer_gamma * outer_own - 0.5 * outer_beta * pseudo.astype(jnp.float32)
    ).astype(jnp.float16)

    flip = jnp.bitwise_xor(me, partner_map[me])
    theirs = lax.switch(
        flip - 1,
        [functools.partial(send, axis="worker", flip=f) for f in range(1, workers)],
        mine,
    )
    own = outer_alpha * momentum.astype(jnp.float32) - (
        0.5 * outer_beta * pseudo.astype(jnp.float32) + 0.5 * outer_gamma * outer_own
    )
    result = (own + theirs.astype(jnp.float32)).astype(jnp.bfloat16)
    parts = [near] if far is None else [near, far]
    raw = jnp.concatenate(
        [
            lax.dot_general(
                weights, p, (((1,), (1,)), ((), ())), preferred_element_type=jnp.float32
            )
            for p in parts
        ],
        axis=1,
    )
    if ring:
        raw = reorder(raw, place)
    raw = raw * scale
    projected = rotate(raw.reshape(BLOCKS, local_pairs, length), cosine, sine, True)
    projected = projected.astype(jnp.bfloat16)
    return (
        projected.reshape(1, BLOCKS, local_pairs, length),
        result.reshape(1, BLOCKS, local_pairs, width),
    )


def solution(mesh):
    return jax.shard_map(
        per_device,
        mesh=mesh,
        in_specs=(
            P("worker", "tensor", None),
            P("worker", None),
            P("worker", None, "tensor", None),
            P(),
            P("worker", None, "tensor", None),
            P("worker", None, "tensor", None),
            P("worker", None, "tensor", None),
            P("worker", None, "tensor", None),
            P("worker", None, "tensor", None),
        ),
        out_specs=(P("worker", None, "tensor", None), P("worker", None, "tensor", None)),
        check_vma=False,
    )
```

```python
import functools
import math

import jax
import jax.numpy as jnp
from jax import lax
from jax.experimental import pallas as pl
from jax.experimental.pallas import tpu as pltpu
from jax.sharding import PartitionSpec as P

KV_HEADS = 4
PAIRS = 64
BLOCKS = 16


rope_base = 1000000.0
clip_norm = 1.0
learn_rate = 0.5
decay_rate = 0.1
bias_first = 1.0
bias_second = 0.632304575
outer_alpha = 0.5
outer_beta = 0.7
outer_gamma = 0.5

TILE = 512
ROWS = 16


def rope_tables(identity, first_pair, count):
    length = identity.shape[0]
    index = jnp.arange(length, dtype=jnp.int32)
    change = jnp.concatenate([jnp.ones((1,), dtype=bool), identity[1:] != identity[:-1]])
    starts = lax.cummax(jnp.where(change, index, jnp.zeros_like(index)), axis=0)
    position = (index - starts).astype(jnp.float32)
    pairs = (first_pair + jnp.arange(count, dtype=jnp.int32)).astype(jnp.float32)
    freq = jnp.exp(pairs * jnp.float32(-math.log(rope_base) / PAIRS))
    angle = freq[:, None] * position[None, :]
    return (jnp.cos(angle), jnp.sin(angle))


def rotate(values, cosine, sine, forward):
    count, length = (values.shape[1], values.shape[2])
    parts = values.reshape(2, KV_HEADS, 2, count, length)
    first = parts[0, :, 0]
    second = parts[0, :, 1]
    cos_b = cosine[None]
    sin_b = sine[None]
    if forward:
        new_first = first * cos_b - second * sin_b
        new_second = second * cos_b + first * sin_b
    else:
        new_first = first * cos_b + second * sin_b
        new_second = second * cos_b - first * sin_b
    keys = jnp.stack([new_first, new_second], axis=1)
    return jnp.concatenate([keys[None], parts[1:2]], axis=0).reshape(BLOCKS, count, length)


def send(values, axis, flip):
    return lax.ppermute(values, axis, [(i, i ^ flip) for i in range(lax.axis_size(axis))])


def swap(values, flip, workers):
    return lax.switch(
        flip - 1,
        [functools.partial(send, axis="worker", flip=f) for f in range(1, workers)],
        values,
    )


def adamw(grad, shrink, first, second, weights, outer):
    half = (0.9 * learn_rate) * first + (0.1 * learn_rate * shrink) * grad
    var = (0.999 / bias_second) * second + (0.001 / bias_second * shrink * shrink) * (grad * grad)
    half = half / (bias_first * (var * lax.rsqrt(var) + 1e-08))
    outer_own = outer.astype(jnp.float32)
    keep = (1.0 - learn_rate * decay_rate) * weights.astype(jnp.float32)
    pseudo = (outer_own - keep + half).astype(jnp.bfloat16).astype(jnp.float32)
    a = (0.5 * outer_gamma) * outer_own
    b = (0.5 * outer_beta) * pseudo
    return a - b, a + b


def limits(mib):
    return pltpu.CompilerParams(vmem_limit_bytes=mib << 20)


def assemble(here, pieces, rows):
    own, x_full, y_low, y_high, d_low, d_high = pieces
    shard = rows.shape[0] // 4

    def put(block, start, ref):
        at = pl.multiple_of((here ^ block) * shard + start, 16)
        rows[pl.ds(at, ref.shape[0]), :] = ref[...]

    put(0, 0, own)
    put(1, 0, x_full)
    put(2, 0, y_low)
    put(2, y_low.shape[0], y_high)
    put(3, 0, d_low)
    put(3, d_low.shape[0], d_high)


def gather_kernel(place, dz, *refs):
    *pieces, grad, squares, rows = refs
    assemble(place[0], pieces, rows)
    part = jnp.dot(dz[...], rows[...], preferred_element_type=jnp.float32)
    grad[...] = part
    part = part * part
    part = jnp.sum(part.reshape(part.shape[0] // 8, 8, part.shape[1]), axis=0)

    @pl.when(pl.program_id(0) == 0)
    def _():
        squares[...] = jnp.zeros_like(squares)

    squares[...] += sum(part[:, 128 * i : 128 * (i + 1)] for i in range(part.shape[1] // 128))


def gather_call(place, dz, pieces):
    width = pieces[0].shape[1]
    columns = dz.shape[0]
    tile = width // 4
    return pl.pallas_call(
        gather_kernel,
        grid_spec=pltpu.PrefetchScalarGridSpec(
            num_scalar_prefetch=1,
            grid=(width // tile,),
            in_specs=[pl.BlockSpec(dz.shape, lambda i, p: (0, 0))]
            + [pl.BlockSpec((x.shape[0], tile), lambda i, p: (0, i)) for x in pieces],
            out_specs=[
                pl.BlockSpec((columns, tile), lambda i, p: (0, i)),
                pl.BlockSpec((8, 128), lambda i, p: (0, 0)),
            ],
            scratch_shapes=[pltpu.VMEM((dz.shape[1], tile), jnp.bfloat16)],
        ),
        out_shape=[
            jax.ShapeDtypeStruct((columns, width), jnp.float32),
            jax.ShapeDtypeStruct((8, 128), jnp.float32),
        ],
        compiler_params=limits(16),
        name="assemble",
    )(place, dz, *pieces)


def adamw_kernel(a, b, c, d, grad, first, second, weights, outer, momentum, mine, own, factor, *,
                 scale):
    @pl.when(pl.program_id(0) == 0)
    def _():
        total = jnp.sum(a[...] + b[...] + c[...] + d[...], axis=(0, 1), keepdims=True)
        norm = jnp.sqrt(total * (scale * scale))
        limit = jnp.minimum(jnp.float32(1.0), clip_norm / (norm + 1e-06))
        factor[0] = limit[0, 0] * scale

    shrink = factor[0]

    def step(i, carry):
        at = (slice(None), pl.ds(pl.multiple_of(i * TILE, TILE), TILE))
        mine[at], rest = adamw(grad[at], shrink, first[at], second[at], weights[at], outer[at])
        own[at] = outer_alpha * momentum[at].astype(jnp.float32) - rest
        return carry

    lax.fori_loop(0, grad.shape[1] // TILE, step, 0, unroll=True)


def adamw_call(sums, grad, arrays, row, rows, scale):
    width = grad.shape[1]
    out = jax.ShapeDtypeStruct((rows, width), jnp.float32)
    fixed = pl.BlockSpec((8, 128), lambda i: (0, 0))
    moved = pl.BlockSpec((ROWS, width), lambda i: (i + row // ROWS, 0))
    return pl.pallas_call(
        functools.partial(adamw_kernel, scale=scale),
        grid=(rows // ROWS,),
        in_specs=[fixed] * 4 + [moved] * 6,
        out_specs=[pl.BlockSpec((ROWS, width), lambda i: (i, 0))] * 2,
        out_shape=[out, out],
        scratch_shapes=[pltpu.SMEM((1,), jnp.float32)],
        compiler_params=limits(12),
        name="adamw",
    )(*sums, grad, *arrays)


def project_kernel(place, weights, cosine, sine, *refs, scale):
    *pieces, projected, rows, raw = refs
    assemble(place[0], pieces, rows)
    part = lax.dot_general(
        weights[...], rows[...], (((1,), (1,)), ((), ())), preferred_element_type=jnp.float32
    )

    @pl.when(pl.program_id(0) == 0)
    def _():
        raw[...] = jnp.zeros_like(raw)

    raw[...] += part

    @pl.when(pl.program_id(0) == pl.num_programs(0) - 1)
    def _():
        count = cosine.shape[0]
        c = cosine[...] * scale
        s = sine[...] * scale
        for head in range(KV_HEADS):
            a = slice(2 * head * count, (2 * head + 1) * count)
            b = slice((2 * head + 1) * count, (2 * head + 2) * count)
            projected[a, :] = (raw[a, :] * c - raw[b, :] * s).astype(jnp.bfloat16)
            projected[b, :] = (raw[b, :] * c + raw[a, :] * s).astype(jnp.bfloat16)
        v = slice(2 * KV_HEADS * count, 4 * KV_HEADS * count)
        projected[v, :] = (raw[v, :] * scale).astype(jnp.bfloat16)


def project_call(place, weights, cosine, sine, pieces, scale):
    columns, width = weights.shape
    length = cosine.shape[1]
    fixed = pl.BlockSpec(cosine.shape, lambda i, p: (0, 0))
    moved = [pl.BlockSpec((x.shape[0], TILE), lambda i, p: (0, i)) for x in (weights, *pieces)]
    return pl.pallas_call(
        functools.partial(project_kernel, scale=scale),
        grid_spec=pltpu.PrefetchScalarGridSpec(
            num_scalar_prefetch=1,
            grid=(width // TILE,),
            in_specs=[moved[0], fixed, fixed] + moved[1:],
            out_specs=pl.BlockSpec((columns, length), lambda i, p: (0, 0)),
            scratch_shapes=[
                pltpu.VMEM((length, TILE), jnp.bfloat16),
                pltpu.VMEM((columns, length), jnp.float32),
            ],
        ),
        out_shape=jax.ShapeDtypeStruct((columns, length), jnp.bfloat16),
        compiler_params=limits(12),
        name="project",
    )(place, weights, cosine, sine, *pieces)


def finish(theirs, own, result, start):
    done = (own + theirs.astype(jnp.float32)).astype(jnp.bfloat16)
    return lax.dynamic_update_slice(result, done, (start, 0))


def per_device(
    hidden_rows,
    document_ids,
    cotangent,
    partner_map,
    inner_weights,
    first_moment,
    second_moment,
    outer_weights,
    outer_momentum,
):
    local_pairs = cotangent.shape[2]
    length = cotangent.shape[3]
    width = hidden_rows.shape[2]
    columns = BLOCKS * local_pairs
    scale = width ** (-0.5)
    shards = lax.axis_size("tensor")
    workers = lax.axis_size("worker")
    place = lax.axis_index("tensor")
    me = lax.axis_index("worker")
    flip = jnp.bitwise_xor(me, partner_map[me])

    hidden = hidden_rows[0]
    weights = inner_weights[0].reshape(columns, width)
    outer = outer_weights[0].reshape(columns, width)
    momentum = outer_momentum[0].reshape(columns, width)
    moment_one = first_moment[0].reshape(columns, width)
    moment_two = second_moment[0].reshape(columns, width)
    cosine, sine = rope_tables(document_ids[0], place * local_pairs, local_pairs)
    dz = (
        rotate(cotangent[0].astype(jnp.float32), cosine, sine, False)
        .astype(jnp.bfloat16)
        .reshape(columns, length)
    )

    if shards == 4 and hidden.shape[0] == 128 and local_pairs == 16 and width % TILE == 0:
        cut = 48
        x_full = send(hidden, "tensor", 1)
        y_high = send(hidden[cut:], "tensor", 2)
        y_low = send(hidden[:cut], "tensor", 2)
        d_high = send(y_high, "tensor", 1)
        d_low = send(x_full[:cut], "tensor", 2)
        dz, flip = lax.optimization_barrier((dz, flip))
        pieces = (hidden, x_full, y_low, y_high, d_low, d_high)
        where = place[None].astype(jnp.int32)
        grad, squares = gather_call(where, dz, pieces)
        sums = [squares] + [send(squares, "tensor", f) for f in (1, 2, 3)]
        arrays = (moment_one, moment_two, weights, outer, momentum)
        sizes = (32, columns - 64, 32)
        starts = (0, 32, columns - 32)

        def tail(f, grad, arrays, pieces):
            theirs = []
            owns = []
            for k in range(3):
                mine, own = adamw_call(sums, grad, arrays, starts[k], sizes[k], scale)
                mine = mine.astype(jnp.float16)
                theirs.append(send(mine, "worker", f))
                owns.append(own)
            projected = project_call(where, weights, cosine, sine, pieces, scale)
            result = jnp.zeros((columns, width), jnp.bfloat16)
            for k in range(2):
                result = finish(theirs[k], owns[k], result, starts[k])
            return projected, result, theirs[2], owns[2]

        projected, result, theirs, own = lax.switch(
            flip - 1, [functools.partial(tail, f) for f in range(1, workers)], grad, arrays, pieces
        )
        result = finish(theirs, own, result, starts[2])
    else:
        gathered = lax.all_gather(hidden, "tensor", axis=0, tiled=True)
        raw = lax.dot_general(
            weights, gathered, (((1,), (1,)), ((), ())), preferred_element_type=jnp.float32
        )
        raw = raw * scale
        projected = rotate(raw.reshape(BLOCKS, local_pairs, length), cosine, sine, True)
        projected = projected.astype(jnp.bfloat16)
        grad = jnp.dot(dz, gathered, preferred_element_type=jnp.float32) * scale
        total = lax.psum(jnp.sum(grad * grad), "tensor")
        factor = jnp.minimum(jnp.float32(1.0), clip_norm / (jnp.sqrt(total) + 1e-06))
        mine, rest = adamw(grad, factor, moment_one, moment_two, weights, outer)
        rest = -rest
        theirs = swap(mine.astype(jnp.float16), flip, workers)
        result = outer_alpha * momentum.astype(jnp.float32) + rest + theirs.astype(jnp.float32)
        result = result.astype(jnp.bfloat16)
    return (
        projected.reshape(1, BLOCKS, local_pairs, length),
        result.reshape(1, BLOCKS, local_pairs, width),
    )


def solution(mesh):
    return jax.shard_map(
        per_device,
        mesh=mesh,
        in_specs=(
            P("worker", "tensor", None),
            P("worker", None),
            P("worker", None, "tensor", None),
            P(),
            P("worker", None, "tensor", None),
            P("worker", None, "tensor", None),
            P("worker", None, "tensor", None),
            P("worker", None, "tensor", None),
            P("worker", None, "tensor", None),
        ),
        out_specs=(P("worker", None, "tensor", None), P("worker", None, "tensor", None)),
        check_vma=False,
    )
```
